32 devices in a mesh: ops: 8 (over y, x, core), grp: 4 (over z).
Axes of the slice: x: 2, y: 2, z: 4, core: 2. Of those that a mesh axis runs over, the one named last changes fastest.
Arguments:
- wave: bfloat16 [32, 512, 512], P(None, 'ops'), may hold values from -12 to 12
- diag_energy: float32 [32, 512, 512], P(None, 'ops'), may hold values from 0.5 to 2
- left_ops: bfloat16 [32, 512, 512], P(('ops', 'grp')), may hold values from -0.1875 to 0.1875
- right_ops: bfloat16 [32, 512, 512], P(('ops', 'grp')), may hold values from -0.25 to 0.25
- pair_sectors: int32 [32, 2], replicated, may hold values from 0 to 31, all different within a row
- sector_slot: int32 [32], replicated, may hold values from 0 to 31, each once
Outputs:
- residual: float32 [32, 512, 512], P(None, 'ops', 'grp')
- sigma_out: float32 [32, 512, 512], P(None, 'ops', 'grp')
The draws below stay inside these ranges and needn't reach their ends.
Inputs may be any that keep to these rules, and one draw needn't show every extreme that they name: `pair_sectors`: each row names two different sectors; every sector is named by some row. `sector_slot`: each slot once.
All inputs are finite; a program needn't handle non-finite values.
Results may differ from the reference program's by a relative error of at most 0.0062.
Values may be sent and summed in bfloat16 or wider, within the bound.
A program may use at most 64 MiB of HBM per device.

```python
import math
import jax
import jax.numpy as jnp
from jax import lax

SECT = 32
BLK = 512
PAIRS = 32


def draw_wave(key, part):
    keys = jax.random.split(key, 1)
    base = jax.random.normal(keys[0], (SECT, BLK, BLK), jnp.float32)
    rows = jnp.arange(BLK, dtype=jnp.float32) / (BLK - 1)
    rising = jnp.sqrt(1.0 + 2.0 * rows)
    value = base * rising[None, :, None]
    return jnp.clip(value, -12.0, 12.0).astype(jnp.bfloat16)


def block_scale(rng, extent, shards, low, top_value):
    factor_of, own = 1.0, jax.random.fold_in(rng, 6)
    for axis_at, blocks in shards:
        steps = jnp.exp(jax.random.uniform(jax.random.fold_in(own, axis_at), (blocks,), jnp.float32, low / len(shards), top_value / len(shards)))
        factor_of = factor_of * jnp.repeat(steps, extent[axis_at] // blocks).reshape([-1 if axis == axis_at else 1 for axis in range(len(extent))])
    return factor_of


def choose_distinct(stream_key, rows, count, top, lift):
    sequence = jax.random.permutation(jax.random.fold_in(stream_key, 1), count)
    favour = sequence
    for power in range(3):
        favour = favour * favour // count
    favour = favour * lift // count
    chance = jax.random.randint(jax.random.fold_in(stream_key, 2), (rows, count), 0, 4096) + favour
    holders = jax.random.permutation(jax.random.fold_in(stream_key, 3), rows)[jnp.arange(count) % rows]
    chance = jnp.where(jnp.arange(rows)[:, None] == holders[None, :], 1 << 14, chance)
    merit = chance * count + jnp.arange(count)
    return lax.top_k(merit.astype(jnp.int32), top)[1].astype(jnp.int32)


def scatter_about(rng, extent, spread, bound, cuts=(), kind=jnp.bfloat16):
    entries = jax.random.normal(rng, extent, jnp.float32) * spread
    if len(cuts) > 0:
        entries = block_scale(rng, extent, cuts, -0.22, 0.18) * entries
    return jnp.clip(entries, min=-bound, max=bound).astype(kind)


def setup_inputs(seed: int = 0) -> dict:
    seeds = jax.random.split(jax.random.key(seed), 7)
    return {
        "wave": draw_wave(jax.random.fold_in(seeds[6], 71), 0),
        "diag_energy": jnp.clip(jnp.exp(math.log(2.0) - 1.3862944 * jax.random.uniform(seeds[1], (SECT, BLK, BLK), jnp.float32) ** block_scale(seeds[1], (SECT, BLK, BLK), ((1, 8),), -0.2, 0.2)), 0.5, 2.0),
        "left_ops": scatter_about(seeds[2], (PAIRS, BLK, BLK), (BLK * 2 * PAIRS // SECT) ** -0.5, 0.1875, ((0, 32),)),
        "right_ops": scatter_about(seeds[3], (PAIRS, BLK, BLK), BLK ** -0.5, 0.25, ((0, 32),)),
        "pair_sectors": choose_distinct(seeds[4], PAIRS, SECT, 2, 512),
        "sector_slot": jax.random.permutation(seeds[5], SECT).astype(jnp.int32),
    }


def apply_pairs(vector, diag_energy, left_ops, right_ops, source, target):
    running = diag_energy * vector.astype(jnp.float32)

    def visit(accum, payload):
        left_op, right_op, from_slot, to_slot = payload
        source_block = lax.dynamic_index_in_dim(vector, from_slot, 0, keepdims=False)
        target_block = lax.dynamic_index_in_dim(vector, to_slot, 0, keepdims=False)
        inner_half = jnp.dot(left_op, source_block, preferred_element_type=jnp.float32).astype(jnp.bfloat16)
        forward = jnp.dot(inner_half, right_op, preferred_element_type=jnp.float32)
        flipped = jnp.dot(left_op.T, target_block, preferred_element_type=jnp.float32).astype(jnp.bfloat16)
        adjoint = jnp.dot(flipped, right_op.T, preferred_element_type=jnp.float32)
        accum = accum.at[to_slot].add(forward)
        accum = accum.at[from_slot].add(adjoint)
        return accum, None

    return lax.scan(visit, running, (left_ops, right_ops, source, target))[0]


def reference(wave, diag_energy, left_ops, right_ops, pair_sectors, sector_slot):
    stored = jnp.take(sector_slot, pair_sectors, axis=0).astype(jnp.int32)
    source = stored[:, 0]
    target = stored[:, 1]
    applied = apply_pairs(wave, diag_energy, left_ops, right_ops, source, target)
    wave_wide = wave.astype(jnp.float32)
    rayleigh = jnp.sum(wave_wide * applied) / jnp.sum(wave_wide * wave_wide)
    residual = applied - rayleigh * wave_wide
    residual_half = residual.astype(jnp.bfloat16)
    sigma_out = apply_pairs(residual_half, diag_energy, left_ops, right_ops, source, target)
    return residual, sigma_out
```

```python
import functools

import jax
import jax.numpy as jnp
from jax import lax
from jax.experimental import pallas as pl
from jax.experimental.pallas import tpu as pltpu
from jax.sharding import PartitionSpec as P

MESH = pl.DeviceIdType.MESH
VMEM = pl.BlockSpec(memory_space=pltpu.VMEM)
SMEM = pl.BlockSpec(memory_space=pltpu.SMEM)
ANY = pl.BlockSpec(memory_space=pl.ANY)


def peer_order(ops_count, grp_count):
    far = sorted(range(grp_count), key=lambda s: -min(s, grp_count - s))
    return [(do, dg) for dg in far for do in range(ops_count) if (do, dg) != (0, 0)]


def greet(shifts, ops_count, grp_count):
    o, g = lax.axis_index("ops"), lax.axis_index("grp")
    barrier = pltpu.get_barrier_semaphore()
    for do, dg in shifts:
        there = (lax.rem(o + do, ops_count), lax.rem(g + dg, grp_count))
        pl.semaphore_signal(barrier, inc=1, device_id=there, device_id_type=MESH)
    pl.semaphore_wait(barrier, len(shifts))


def fetch_kernel(ops_count, out_ref_rows, outgoing, blocks, send_sem, recv_sem, own_sem):
    o, g = lax.axis_index("ops"), lax.axis_index("grp")
    rows = out_ref_rows
    shifts = [(do, 0) for do in range(1, ops_count)]
    mine = blocks.at[:, pl.ds(pl.multiple_of(o * rows, rows), rows), :]
    own = pltpu.make_async_copy(outgoing.at[o], mine, own_sem)
    own.start()
    greet(shifts, ops_count, lax.axis_size("grp"))
    copies = []
    for n, (do, _) in enumerate(shifts):
        to = lax.rem(o + do, ops_count)
        copy = pltpu.make_async_remote_copy(
            src_ref=outgoing.at[to], dst_ref=mine,
            send_sem=send_sem.at[n], recv_sem=recv_sem.at[n],
            device_id=(to, g), device_id_type=MESH,
        )
        copy.start()
        copies.append(copy)
    own.wait()
    for copy in copies:
        copy.wait()


def scatter_kernel(ops_count, grp_count, rows, cols, with_stats, *refs):
    if with_stats:
        blocks, stats, pieces, all_stats, send_sem, recv_sem, own_sem, ssend, srecv = refs
    else:
        blocks, pieces, send_sem, recv_sem, own_sem = refs
    o, g = lax.axis_index("ops"), lax.axis_index("grp")
    me = o * grp_count + g
    shifts = peer_order(ops_count, grp_count)

    def part(to_o, to_g):
        return blocks.at[
            :,
            pl.ds(pl.multiple_of(to_o * rows, rows), rows),
            pl.ds(pl.multiple_of(to_g * cols, cols), cols),
        ]

    waits = [pltpu.make_async_copy(part(o, g), pieces.at[me], own_sem.at[0])]
    if with_stats:
        waits.append(pltpu.make_async_copy(stats, all_stats.at[me], own_sem.at[1]))
    for copy in waits:
        copy.start()
    greet(shifts, ops_count, grp_count)
    for n, (do, dg) in enumerate(shifts):
        there = (lax.rem(o + do, ops_count), lax.rem(g + dg, grp_count))
        if with_stats:
            copy = pltpu.make_async_remote_copy(
                src_ref=stats, dst_ref=all_stats.at[me],
                send_sem=ssend.at[n], recv_sem=srecv.at[n],
                device_id=there, device_id_type=MESH,
            )
            copy.start()
            waits.append(copy)
        copy = pltpu.make_async_remote_copy(
            src_ref=part(*there), dst_ref=pieces.at[me],
            send_sem=send_sem.at[n], recv_sem=recv_sem.at[n],
            device_id=there, device_id_type=MESH,
        )
        copy.start()
        waits.append(copy)
    for copy in waits:
        copy.wait()


def collect_kernel(ops_count, grp_count, rows, cols, pieces, blocks, send_sem, recv_sem, own_sem):
    o, g = lax.axis_index("ops"), lax.axis_index("grp")
    shifts = peer_order(ops_count, grp_count)
    mine = blocks.at[
        :,
        pl.ds(pl.multiple_of(o * rows, rows), rows),
        pl.ds(pl.multiple_of(g * cols, cols), cols),
    ]
    waits = [pltpu.make_async_copy(pieces.at[o * grp_count + g], mine, own_sem)]
    waits[0].start()
    greet(shifts, ops_count, grp_count)
    for n, (do, dg) in enumerate(shifts):
        to_o, to_g = lax.rem(o + do, ops_count), lax.rem(g + dg, grp_count)
        copy = pltpu.make_async_remote_copy(
            src_ref=pieces.at[to_o * grp_count + to_g], dst_ref=mine,
            send_sem=send_sem.at[n], recv_sem=recv_sem.at[n],
            device_id=(to_o, to_g), device_id_type=MESH,
        )
        copy.start()
        waits.append(copy)
    for copy in waits:
        copy.wait()


def slot_of(pair_ref, slot_ref, side, pair):
    return slot_ref[pair_ref[side, pair]]


def stage_kernel(ops_count, grp_count, pair_dev, pair_ref, slot_ref, wave, outgoing):
    g = lax.axis_index("grp")
    for to in range(ops_count):
        for j in range(pair_dev):
            pair = (to * grp_count + g) * pair_dev + j
            for side in range(2):
                outgoing[to, 2 * j + side] = wave[slot_of(pair_ref, slot_ref, side, pair)]


def fold(value):
    rows, width = value.shape
    tall = jnp.sum(value.reshape(rows // 8, 8, width), axis=0)
    total = tall[:, :128]
    for c in range(1, width // 128):
        total = total + tall[:, c * 128:(c + 1) * 128]
    return total


def pair_products(left, right, source, target):
    inner = jnp.dot(left, source, preferred_element_type=jnp.float32).astype(jnp.bfloat16)
    forward = jnp.dot(inner, right, preferred_element_type=jnp.float32)
    flipped = lax.dot_general(
        left, target, (((0,), (0,)), ((), ())), preferred_element_type=jnp.float32
    ).astype(jnp.bfloat16)
    adjoint = lax.dot_general(
        flipped, right, (((1,), (1,)), ((), ())), preferred_element_type=jnp.float32
    )
    return forward, adjoint


def pairs_kernel(pair_dev, with_stats, *refs):
    if with_stats:
        blocks, left, right, diag, wave, out, stats = refs
        cross = jnp.zeros((8, 128), jnp.float32)
    else:
        blocks, left, right, out = refs
    for j in range(pair_dev):
        source, target = blocks[2 * j], blocks[2 * j + 1]
        forward, adjoint = pair_products(left[j], right[j], source, target)
        out[2 * j] = forward.astype(jnp.bfloat16)
        out[2 * j + 1] = adjoint.astype(jnp.bfloat16)
        if with_stats:
            cross = cross + fold(target.astype(jnp.float32) * forward)
            cross = cross + fold(source.astype(jnp.float32) * adjoint)
    if with_stats:
        zero = jnp.zeros((8, 128), jnp.float32)

        def visit(k, carry):
            top, norm = carry
            v = wave[k].astype(jnp.float32)
            square = v * v
            return top + fold(diag[k] * square), norm + fold(square)

        top, norm = lax.fori_loop(0, wave.shape[0], visit, (zero, zero))
        stats[0] = top + cross
        stats[1] = norm


def add_pieces(pair_ref, slot_ref, pieces, total):
    devices, held = pieces.shape[:2]
    pair_dev = held // 2

    def visit(d, carry):
        for j in range(pair_dev):
            pair = d * pair_dev + j
            for side in range(2):
                k = slot_of(pair_ref, slot_ref, 1 - side, pair)
                total[k] = total[k] + pieces[d, 2 * j + side].astype(jnp.float32)
        return carry

    lax.fori_loop(0, devices, visit, 0)


def residual_kernel(pair_ref, slot_ref, pieces, all_stats, diag, wave, residual, half, outgoing):
    sectors = wave.shape[0]

    def start(k, carry):
        residual[k] = diag[k] * wave[k].astype(jnp.float32)
        return carry

    lax.fori_loop(0, sectors, start, 0)
    add_pieces(pair_ref, slot_ref, pieces, residual)
    sums = jnp.sum(all_stats[...], axis=0)
    rayleigh = jnp.sum(sums[0]) / jnp.sum(sums[1])

    def finish(k, carry):
        value = residual[k] - rayleigh * wave[k].astype(jnp.float32)
        residual[k] = value
        half[k] = value.astype(jnp.bfloat16)
        return carry

    lax.fori_loop(0, sectors, finish, 0)
    devices, held = outgoing.shape[:2]
    pair_dev = held // 2

    def hand_out(d, carry):
        for j in range(pair_dev):
            for side in range(2):
                k = slot_of(pair_ref, slot_ref, side, d * pair_dev + j)
                outgoing[d, 2 * j + side] = half[k]
        return carry

    lax.fori_loop(0, devices, hand_out, 0)


def sigma_kernel(pair_ref, slot_ref, pieces, diag, half, sigma):
    def start(k, carry):
        sigma[k] = diag[k] * half[k].astype(jnp.float32)
        return carry

    lax.fori_loop(0, half.shape[0], start, 0)
    add_pieces(pair_ref, slot_ref, pieces, sigma)


def dma(count):
    return pltpu.SemaphoreType.DMA((count,))


def direct_body(wave, diag_energy, left_ops, right_ops, pair_sectors, sector_slot):
    ops_count, grp_count = lax.axis_size("ops"), lax.axis_size("grp")
    sectors, rows, width = wave.shape
    height = rows * ops_count
    pair_dev = left_ops.shape[0]
    cols = width // grp_count
    devices = ops_count * grp_count
    peers = devices - 1
    half_t, wide_t = jnp.bfloat16, jnp.float32
    shape = jax.ShapeDtypeStruct
    pair_sides = pair_sectors.T
    start = lax.axis_index("grp") * cols
    diag = lax.dynamic_slice_in_dim(diag_energy, start, cols, 2)
    wave_share = lax.dynamic_slice_in_dim(wave, start, cols, 2)

    outgoing = pl.pallas_call(
        functools.partial(stage_kernel, ops_count, grp_count, pair_dev),
        out_shape=shape((ops_count, 2 * pair_dev, rows, width), half_t),
        in_specs=[SMEM, SMEM, VMEM], out_specs=VMEM, name="stage",
    )(pair_sides, sector_slot, wave)
    blocks = pl.pallas_call(
        functools.partial(fetch_kernel, ops_count, rows),
        out_shape=shape((2 * pair_dev, height, width), half_t),
        in_specs=[ANY], out_specs=ANY, name="fetch",
        scratch_shapes=[dma(ops_count - 1), dma(ops_count - 1), pltpu.SemaphoreType.DMA],
        compiler_params=pltpu.CompilerParams(collective_id=0, has_side_effects=True),
    )(outgoing)
    partial_blocks, stats = pl.pallas_call(
        functools.partial(pairs_kernel, pair_dev, True),
        out_shape=(shape((2 * pair_dev, height, width), half_t), shape((2, 8, 128), wide_t)),
        in_specs=[VMEM] * 5, out_specs=(VMEM, VMEM), name="pairs_first",
    )(blocks, left_ops, right_ops, diag, wave_share)
    pieces, all_stats = pl.pallas_call(
        functools.partial(scatter_kernel, ops_count, grp_count, rows, cols, True),
        out_shape=(
            shape((devices, 2 * pair_dev, rows, cols), half_t),
            shape((devices, 2, 8, 128), wide_t),
        ),
        in_specs=[ANY, ANY], out_specs=(ANY, ANY), name="scatter_first",
        scratch_shapes=[dma(peers), dma(peers), dma(2), dma(peers), dma(peers)],
        compiler_params=pltpu.CompilerParams(collective_id=1, has_side_effects=True),
    )(partial_blocks, stats)
    residual, residual_half, handed = pl.pallas_call(
        residual_kernel,
        out_shape=(
            shape((sectors, rows, cols), wide_t),
            shape((sectors, rows, cols), half_t),
            shape((devices, 2 * pair_dev, rows, cols), half_t),
        ),
        in_specs=[SMEM, SMEM] + [VMEM] * 4, out_specs=(VMEM,) * 3, name="residual",
    )(pair_sides, sector_slot, pieces, all_stats, diag, wave_share)
    blocks = pl.pallas_call(
        functools.partial(collect_kernel, ops_count, grp_count, rows, cols),
        out_shape=shape((2 * pair_dev, height, width), half_t),
        in_specs=[ANY], out_specs=ANY, name="collect",
        scratch_shapes=[dma(peers), dma(peers), pltpu.SemaphoreType.DMA],
        compiler_params=pltpu.CompilerParams(collective_id=2, has_side_effects=True),
    )(handed)
    partial_blocks = pl.pallas_call(
        functools.partial(pairs_kernel, pair_dev, False),
        out_shape=shape((2 * pair_dev, height, width), half_t),
        in_specs=[VMEM] * 3, out_specs=VMEM, name="pairs_second",
    )(blocks, left_ops, right_ops)
    pieces = pl.pallas_call(
        functools.partial(scatter_kernel, ops_count, grp_count, rows, cols, False),
        out_shape=shape((devices, 2 * pair_dev, rows, cols), half_t),
        in_specs=[ANY], out_specs=ANY, name="scatter_second",
        scratch_shapes=[dma(peers), dma(peers), dma(1)],
        compiler_params=pltpu.CompilerParams(collective_id=3, has_side_effects=True),
    )(partial_blocks)
    sigma_out = pl.pallas_call(
        sigma_kernel,
        out_shape=shape((sectors, rows, cols), wide_t),
        in_specs=[SMEM, SMEM] + [VMEM] * 3, out_specs=VMEM, name="sigma",
    )(pair_sides, sector_slot, pieces, diag, residual_half)
    return residual, sigma_out


def segment_total(received, targets, sectors):
    choose = (targets[None, :] == jnp.arange(sectors, dtype=jnp.int32)[:, None]).astype(jnp.float32)
    return jnp.dot(
        choose, received, precision=lax.Precision.HIGHEST, preferred_element_type=jnp.float32
    )


def apply_pairs(vector, left_ops, right_ops, wanted):
    ops_count = lax.axis_size("ops")
    sectors, rows_here, block_width = vector.shape
    pair_dev = left_ops.shape[0]
    cell_count = rows_here * block_width
    outgoing = jnp.take(vector, wanted.reshape(-1), axis=0).reshape(
        ops_count, pair_dev * 2, rows_here, block_width
    )
    fetched = lax.all_to_all(outgoing, "ops", split_axis=0, concat_axis=2, tiled=True)
    inner_half = jnp.einsum(
        "pij,pjk->pik", left_ops, fetched[:, 0], preferred_element_type=jnp.float32
    ).astype(jnp.bfloat16)
    forward = jnp.einsum("pik,pkl->pil", inner_half, right_ops, preferred_element_type=jnp.float32)
    flipped = jnp.einsum(
        "pji,pjk->pik", left_ops, fetched[:, 1], preferred_element_type=jnp.float32
    ).astype(jnp.bfloat16)
    adjoint = jnp.einsum("pik,plk->pil", flipped, right_ops, preferred_element_type=jnp.float32)
    forward_parts = lax.all_to_all(
        forward.reshape(pair_dev, ops_count, rows_here, block_width),
        "ops",
        split_axis=1,
        concat_axis=1,
        tiled=True,
    )
    adjoint_parts = lax.all_to_all(
        adjoint.reshape(pair_dev, ops_count, rows_here, block_width),
        "ops",
        split_axis=1,
        concat_axis=1,
        tiled=True,
    )
    summed = segment_total(
        forward_parts.reshape(-1, cell_count), wanted[:, :, 1].T.reshape(-1), sectors
    )
    summed = summed + segment_total(
        adjoint_parts.reshape(-1, cell_count), wanted[:, :, 0].T.reshape(-1), sectors
    )
    return summed.reshape(sectors, rows_here, block_width)


def reduce_group(partial_value):
    return lax.psum_scatter(partial_value, "grp", scatter_dimension=2, tiled=True)


def collective_body(wave, diag_energy, left_ops, right_ops, pair_sectors, sector_slot):
    ops_count = lax.axis_size("ops")
    grp_count = lax.axis_size("grp")
    pair_dev = left_ops.shape[0]
    block_width = wave.shape[2]
    stored = jnp.take(sector_slot, pair_sectors, axis=0).reshape(ops_count, grp_count, pair_dev, 2)
    wanted = lax.dynamic_index_in_dim(stored, lax.axis_index("grp"), 1, keepdims=False)
    column_share = block_width // grp_count
    column_start = lax.axis_index("grp") * column_share
    applied_sum = reduce_group(apply_pairs(wave, left_ops, right_ops, wanted))
    wave_wide = wave.astype(jnp.float32)
    diag_share = lax.dynamic_slice_in_dim(diag_energy, column_start, column_share, 2)
    wave_share = lax.dynamic_slice_in_dim(wave_wide, column_start, column_share, 2)
    applied = diag_share * wave_share + applied_sum
    products = lax.psum(
        (jnp.sum(wave_share * applied), jnp.sum(wave_share * wave_share)), ("ops", "grp")
    )
    rayleigh = products[0] / products[1]
    residual = applied - rayleigh * wave_share
    residual_half = residual.astype(jnp.bfloat16)
    full_half = lax.all_gather(residual_half, "grp", axis=2, tiled=True)
    second = reduce_group(apply_pairs(full_half, left_ops, right_ops, wanted))
    sigma_out = diag_share * residual_half.astype(jnp.float32) + second
    return (residual, sigma_out)


def solution(mesh):
    rows_tile, lane_tile, most_peers = 16, 128, 64

    def body(wave, diag_energy, left_ops, right_ops, pair_sectors, sector_slot):
        rows, width = wave.shape[1:]
        fits = rows % rows_tile == 0 and width % (lane_tile * mesh.shape["grp"]) == 0
        chosen = direct_body if fits and mesh.size <= most_peers else collective_body
        return chosen(wave, diag_energy, left_ops, right_ops, pair_sectors, sector_slot)

    return jax.shard_map(
        body,
        mesh=mesh,
        in_specs=(
            P(None, "ops", None),
            P(None, "ops", None),
            P(("ops", "grp"), None, None),
            P(("ops", "grp"), None, None),
            P(),
            P(),
        ),
        out_specs=(P(None, "ops", "grp"), P(None, "ops", "grp")),
        check_vma=False,
    )
```

```python
import functools

import jax
import jax.numpy as jnp
from jax import lax
from jax.experimental import pallas as pl
from jax.experimental.pallas import tpu as pltpu
from jax.sharding import PartitionSpec as P

MESH = pl.DeviceIdType.MESH
VMEM = pl.BlockSpec(memory_space=pltpu.VMEM)
SMEM = pl.BlockSpec(memory_space=pltpu.SMEM)
ANY = pl.BlockSpec(memory_space=pl.ANY)


def chain_kernel(pair_sides, sector_slot, slots, previous, keep, last):
    pairs = pair_sides.shape[1]
    sectors = sector_slot.shape[0]

    def clear(k, carry):
        last[k] = -1
        return carry

    lax.fori_loop(0, sectors, clear, 0)
    for side in range(2):

        def visit(p, carry, side=side):
            item = side * pairs + p
            slots[item] = sector_slot[pair_sides[side, p]]
            k = sector_slot[pair_sides[1 - side, p]]
            before = last[k]
            previous[item] = jnp.maximum(before, 0)
            keep[item] = jnp.where(before >= 0, 1.0, 0.0)
            last[k] = item
            return carry

        lax.fori_loop(0, pairs, visit, 0)


def fold(value):
    rows, width = value.shape
    tall = jnp.sum(value.reshape(rows // 8, 8, width), axis=0)
    total = tall[:, :128]
    for c in range(1, width // 128):
        total = total + tall[:, c * 128:(c + 1) * 128]
    return total


def product(side, left, right, block):
    half = lax.dot_general(
        left, block, (((1 - side,), (0,)), ((), ())), preferred_element_type=jnp.float32
    ).astype(jnp.bfloat16)
    return lax.dot_general(
        half, right, (((1,), (side,)), ((), ())), preferred_element_type=jnp.float32
    )


def whole_kernel(
    ops_count, grp_count, pair_dev,
    slots, previous, keep, last, wave_in, diag_in, left_in, right_in,
    residual_out, sigma_out,
    wave, diag, left, right, send_a, blocks_a, out_b, pieces_b, send_c, blocks_c,
    out_d, pieces_d, run, residual, half, sigma, stats, all_stats,
    load_sem, own_sem, send_sem, recv_sem,
):
    o, g = lax.axis_index("ops"), lax.axis_index("grp")
    me = o * grp_count + g
    devices = ops_count * grp_count
    pairs = devices * pair_dev
    sectors, rows, width = wave.shape
    cols = width // grp_count
    wide = jnp.float32
    far_first = sorted(range(grp_count), key=lambda s: -min(s, grp_count - s))
    my_cols = pl.ds(pl.multiple_of(g * cols, cols), cols)

    def each_peer(visit):
        for dg in far_first:

            def step(do, carry, dg=dg):
                visit(lax.rem(o + do, ops_count), lax.rem(g + dg, grp_count))
                return carry

            lax.fori_loop(1 if dg == 0 else 0, ops_count, step, 0)

    def place(ref, side, at_o, at_g):
        return ref.at[
            side, :,
            pl.ds(pl.multiple_of(at_o * rows, rows), rows),
            pl.ds(pl.multiple_of(at_g * cols, cols), cols),
        ]

    def send(group, source, target, to_o, to_g):
        pltpu.make_async_remote_copy(
            src_ref=source, dst_ref=target,
            send_sem=send_sem.at[group], recv_sem=recv_sem.at[group],
            device_id=(to_o, to_g), device_id_type=MESH,
        ).start()

    def whole_of(group, like):
        return pltpu.make_async_remote_copy(
            src_ref=like, dst_ref=like,
            send_sem=send_sem.at[group], recv_sem=recv_sem.at[group],
            device_id=(lax.rem(o + 1, ops_count), g), device_id_type=MESH,
        )

    loads = [
        pltpu.make_async_copy(wave_in, wave, load_sem.at[0]),
        pltpu.make_async_copy(left_in, left, load_sem.at[1]),
        pltpu.make_async_copy(right_in, right, load_sem.at[2]),
        pltpu.make_async_copy(diag_in.at[:, :, my_cols], diag, load_sem.at[3]),
    ]
    for load in loads:
        load.start()
    barrier = pltpu.get_barrier_semaphore()
    each_peer(
        lambda to_o, to_g: pl.semaphore_signal(
            barrier, inc=1, device_id=(to_o, to_g), device_id_type=MESH
        )
    )

    loads[0].wait()

    def stage(side):
        for to in range(ops_count):
            for j in range(pair_dev):
                pair = (to * grp_count + g) * pair_dev + j
                send_a[side, to, j] = wave[slots[side * pairs + pair]]

    fetch_groups, own = (0, 1), []
    stage(0)
    pl.semaphore_wait(barrier, devices - 1)
    my_rows = pl.ds(pl.multiple_of(o * rows, rows), rows)
    for side in range(2):
        if side == 1:
            stage(1)

        def fetch(do, carry, side=side):
            to = lax.rem(o + do, ops_count)
            send(fetch_groups[side], send_a.at[side, to], blocks_a.at[side, :, my_rows, :], to, g)
            return carry

        lax.fori_loop(1, ops_count, fetch, 0)
        own.append(
            pltpu.make_async_copy(
                send_a.at[side, o], blocks_a.at[side, :, my_rows, :], own_sem.at[side]
            )
        )
        own[side].start()

    loads[3].wait()
    zero = jnp.zeros((8, 128), wide)

    def tally(k, carry):
        value = wave[k, :, my_cols].astype(wide)
        square = value * value
        return carry[0] + fold(diag[k] * square), carry[1] + fold(square)

    top, norm = lax.fori_loop(0, sectors, tally, (zero, zero))
    loads[1].wait()
    loads[2].wait()

    def arrive(group, like):
        whole_of(group, like).wait_recv()

    def leave(group, like):
        whole_of(group, like).wait_send()

    fetch_like = [blocks_a.at[s, :, pl.ds(0, (ops_count - 1) * rows), :] for s in range(2)]
    like_b = [pieces_b.at[s, pl.ds(0, (devices - 1) * pair_dev)] for s in range(2)]
    like_c = [send_c.at[s, pl.ds(0, (devices - 1) * pair_dev)] for s in range(2)]
    like_d = [pieces_d.at[s, pl.ds(0, (devices - 1) * pair_dev)] for s in range(2)]
    stats_like = all_stats.at[pl.ds(0, devices - 1)]
    my_pairs = pl.ds(me * pair_dev, pair_dev)

    def scatter(side, group, out, pieces):
        copy = pltpu.make_async_copy(
            place(out, side, o, g), pieces.at[side, my_pairs], own_sem.at[group]
        )
        copy.start()
        each_peer(
            lambda to_o, to_g: send(
                group, place(out, side, to_o, to_g), pieces.at[side, my_pairs], to_o, to_g
            )
        )
        return copy

    for side in range(2):
        arrive(fetch_groups[side], fetch_like[side])
        own[side].wait()
        if side == 1:
            for j in range(pair_dev):
                value = product(1, left[j], right[j], blocks_a[1, j])
                out_b[1, j] = value.astype(jnp.bfloat16)
                top = top + fold(blocks_a[0, j].astype(wide) * value)
                top = top + fold(blocks_a[1, j].astype(wide) * out_f[j])
            stats[0] = top
            stats[1] = norm
            own.append(pltpu.make_async_copy(stats, all_stats.at[me], own_sem.at[8]))
            own[-1].start()
            each_peer(lambda to_o, to_g: send(8, stats, all_stats.at[me], to_o, to_g))
        else:
            out_f = []
            for j in range(pair_dev):
                value = product(0, left[j], right[j], blocks_a[0, j])
                out_b[0, j] = value.astype(jnp.bfloat16)
                out_f.append(value)
        own.append(scatter(side, 2 + side, out_b, pieces_b))

    def chain(pieces):
        for side in range(2):

            def visit(p, carry, side=side):
                item = side * pairs + p
                run[item] = pieces[side, p].astype(wide) + keep[item] * run[previous[item]]
                return carry

            lax.fori_loop(0, pairs, visit, 0)

    for copy in own[2:]:
        copy.wait()
    for side in range(2):
        arrive(2 + side, like_b[side])
    arrive(8, stats_like)
    run[0] = jnp.zeros((rows, cols), wide)
    chain(pieces_b)
    sums = jnp.sum(all_stats[...], axis=0)
    rayleigh = jnp.sum(sums[0]) / jnp.sum(sums[1])

    def finish(k, carry):
        value = (diag[k] - rayleigh) * wave[k, :, my_cols].astype(wide) + run[last[k]]
        residual[k] = value
        half[k] = value.astype(jnp.bfloat16)
        return carry

    lax.fori_loop(0, sectors, finish, 0)
    residual_copy = pltpu.make_async_copy(residual, residual_out, load_sem.at[0])
    residual_copy.start()

    own = []
    for side in range(2):

        def hand_out(p, carry, side=side):
            send_c[side, p] = half[slots[side * pairs + p]]
            return carry

        lax.fori_loop(0, pairs, hand_out, 0)

        def collect(to_o, to_g, side=side):
            to = to_o * grp_count + to_g
            source = send_c.at[side, pl.ds(to * pair_dev, pair_dev)]
            send(4 + side, source, place(blocks_c, side, o, g), to_o, to_g)

        each_peer(collect)
        own.append(
            pltpu.make_async_copy(
                send_c.at[side, my_pairs], place(blocks_c, side, o, g), own_sem.at[4 + side]
            )
        )
        own[side].start()
    for side in range(2):
        own[side].wait()
        arrive(4 + side, like_c[side])
        for j in range(pair_dev):
            value = product(side, left[j], right[j], blocks_c[side, j])
            out_d[side, j] = value.astype(jnp.bfloat16)
        own.append(scatter(side, 6 + side, out_d, pieces_d))
    for side in range(2):
        own[2 + side].wait()
        arrive(6 + side, like_d[side])
    run[0] = jnp.zeros((rows, cols), wide)
    chain(pieces_d)

    def close(k, carry):
        sigma[k] = diag[k] * half[k].astype(wide) + run[last[k]]
        return carry

    lax.fori_loop(0, sectors, close, 0)
    sigma_copy = pltpu.make_async_copy(sigma, sigma_out, load_sem.at[1])
    sigma_copy.start()
    for side in range(2):
        leave(side, fetch_like[side])
        leave(2 + side, like_b[side])
        leave(4 + side, like_c[side])
        leave(6 + side, like_d[side])
    leave(8, stats_like)
    residual_copy.wait()
    sigma_copy.wait()


def direct_body(wave, diag_energy, left_ops, right_ops, pair_sectors, sector_slot):
    ops_count, grp_count = lax.axis_size("ops"), lax.axis_size("grp")
    sectors, rows, width = wave.shape
    height = rows * ops_count
    pair_dev = left_ops.shape[0]
    pairs = pair_sectors.shape[0]
    cols = width // grp_count
    devices = ops_count * grp_count
    thin, wide = jnp.bfloat16, jnp.float32
    shape = jax.ShapeDtypeStruct
    chains = pl.pallas_call(
        chain_kernel,
        out_shape=(
            shape((2 * pairs,), jnp.int32), shape((2 * pairs,), jnp.int32),
            shape((2 * pairs,), wide), shape((sectors,), jnp.int32),
        ),
        in_specs=[SMEM, SMEM], out_specs=(SMEM,) * 4, name="chain",
    )(pair_sectors.T, sector_slot)
    blocks = (2, pair_dev, height, width)
    pieces = (2, pairs, rows, cols)
    share = (sectors, rows, cols)
    return pl.pallas_call(
        functools.partial(whole_kernel, ops_count, grp_count, pair_dev),
        out_shape=(shape(share, wide), shape(share, wide)),
        in_specs=[SMEM] * 4 + [ANY] * 4, out_specs=(ANY, ANY), name="whole",
        scratch_shapes=[
            pltpu.VMEM(wave.shape, thin), pltpu.VMEM(share, wide),
            pltpu.VMEM(left_ops.shape, thin), pltpu.VMEM(right_ops.shape, thin),
            pltpu.VMEM((2, ops_count, pair_dev, rows, width), thin), pltpu.VMEM(blocks, thin),
            pltpu.VMEM(blocks, thin), pltpu.VMEM(pieces, thin),
            pltpu.VMEM(pieces, thin), pltpu.VMEM(blocks, thin),
            pltpu.VMEM(blocks, thin), pltpu.VMEM(pieces, thin),
            pltpu.VMEM((2 * pairs, rows, cols), wide), pltpu.VMEM(share, wide),
            pltpu.VMEM(share, thin), pltpu.VMEM(share, wide),
            pltpu.VMEM((2, 8, 128), wide), pltpu.VMEM((devices, 2, 8, 128), wide),
            pltpu.SemaphoreType.DMA((4,)), pltpu.SemaphoreType.DMA((9,)),
            pltpu.SemaphoreType.DMA((9,)), pltpu.SemaphoreType.DMA((9,)),
        ],
        compiler_params=pltpu.CompilerParams(
            collective_id=0, has_side_effects=True, vmem_limit_bytes=48 << 20
        ),
    )(*chains, wave, diag_energy, left_ops, right_ops)


def segment_total(received, targets, sectors):
    choose = (targets[None, :] == jnp.arange(sectors, dtype=jnp.int32)[:, None]).astype(jnp.float32)
    return jnp.dot(
        choose, received, precision=lax.Precision.HIGHEST, preferred_element_type=jnp.float32
    )


def apply_pairs(vector, left_ops, right_ops, wanted):
    ops_count = lax.axis_size("ops")
    sectors, rows_here, block_width = vector.shape
    pair_dev = left_ops.shape[0]
    cell_count = rows_here * block_width
    outgoing = jnp.take(vector, wanted.reshape(-1), axis=0).reshape(
        ops_count, pair_dev * 2, rows_here, block_width
    )
    fetched = lax.all_to_all(outgoing, "ops", split_axis=0, concat_axis=2, tiled=True)
    inner_half = jnp.einsum(
        "pij,pjk->pik", left_ops, fetched[:, 0], preferred_element_type=jnp.float32
    ).astype(jnp.bfloat16)
    forward = jnp.einsum("pik,pkl->pil", inner_half, right_ops, preferred_element_type=jnp.float32)
    flipped = jnp.einsum(
        "pji,pjk->pik", left_ops, fetched[:, 1], preferred_element_type=jnp.float32
    ).astype(jnp.bfloat16)
    adjoint = jnp.einsum("pik,plk->pil", flipped, right_ops, preferred_element_type=jnp.float32)
    forward_parts = lax.all_to_all(
        forward.reshape(pair_dev, ops_count, rows_here, block_width),
        "ops",
        split_axis=1,
        concat_axis=1,
        tiled=True,
    )
    adjoint_parts = lax.all_to_all(
        adjoint.reshape(pair_dev, ops_count, rows_here, block_width),
        "ops",
        split_axis=1,
        concat_axis=1,
        tiled=True,
    )
    summed = segment_total(
        forward_parts.reshape(-1, cell_count), wanted[:, :, 1].T.reshape(-1), sectors
    )
    summed = summed + segment_total(
        adjoint_parts.reshape(-1, cell_count), wanted[:, :, 0].T.reshape(-1), sectors
    )
    return summed.reshape(sectors, rows_here, block_width)


def reduce_group(partial_value):
    return lax.psum_scatter(partial_value, "grp", scatter_dimension=2, tiled=True)


def collective_body(wave, diag_energy, left_ops, right_ops, pair_sectors, sector_slot):
    ops_count = lax.axis_size("ops")
    grp_count = lax.axis_size("grp")
    pair_dev = left_ops.shape[0]
    block_width = wave.shape[2]
    stored = jnp.take(sector_slot, pair_sectors, axis=0).reshape(ops_count, grp_count, pair_dev, 2)
    wanted = lax.dynamic_index_in_dim(stored, lax.axis_index("grp"), 1, keepdims=False)
    column_share = block_width // grp_count
    column_start = lax.axis_index("grp") * column_share
    applied_sum = reduce_group(apply_pairs(wave, left_ops, right_ops, wanted))
    wave_wide = wave.astype(jnp.float32)
    diag_share = lax.dynamic_slice_in_dim(diag_energy, column_start, column_share, 2)
    wave_share = lax.dynamic_slice_in_dim(wave_wide, column_start, column_share, 2)
    applied = diag_share * wave_share + applied_sum
    products = lax.psum(
        (jnp.sum(wave_share * applied), jnp.sum(wave_share * wave_share)), ("ops", "grp")
    )
    rayleigh = products[0] / products[1]
    residual = applied - rayleigh * wave_share
    residual_half = residual.astype(jnp.bfloat16)
    full_half = lax.all_gather(residual_half, "grp", axis=2, tiled=True)
    second = reduce_group(apply_pairs(full_half, left_ops, right_ops, wanted))
    sigma_out = diag_share * residual_half.astype(jnp.float32) + second
    return (residual, sigma_out)


def solution(mesh):
    rows_tile, lane_tile, most_peers = 16, 128, 64

    def body(wave, diag_energy, left_ops, right_ops, pair_sectors, sector_slot):
        rows, width = wave.shape[1:]
        fits = rows % rows_tile == 0 and width % (lane_tile * mesh.shape["grp"]) == 0
        chosen = direct_body if fits and mesh.size <= most_peers else collective_body
        return chosen(wave, diag_energy, left_ops, right_ops, pair_sectors, sector_slot)

    return jax.shard_map(
        body,
        mesh=mesh,
        in_specs=(
            P(None, "ops", None),
            P(None, "ops", None),
            P(("ops", "grp"), None, None),
            P(("ops", "grp"), None, None),
            P(),
            P(),
        ),
        out_specs=(P(None, "ops", "grp"), P(None, "ops", "grp")),
        check_vma=False,
    )
```

```python
import functools

import jax
import jax.numpy as jnp
from jax import lax
from jax.experimental import pallas as pl
from jax.experimental.pallas import tpu as pltpu
from jax.sharding import PartitionSpec as P

MESH = pl.DeviceIdType.MESH
VMEM = pl.BlockSpec(memory_space=pltpu.VMEM)
SMEM = pl.BlockSpec(memory_space=pltpu.SMEM)
ANY = pl.BlockSpec(memory_space=pl.ANY)


def chain_kernel(pair_sides, sector_slot, slots, previous, keep, last):
    pairs = pair_sides.shape[1]
    sectors = sector_slot.shape[0]

    def clear(k, carry):
        last[k] = -1
        return carry

    lax.fori_loop(0, sectors, clear, 0)
    for side in range(2):

        def visit(p, carry, side=side):
            item = side * pairs + p
            slots[item] = sector_slot[pair_sides[side, p]]
            k = sector_slot[pair_sides[1 - side, p]]
            before = last[k]
            previous[item] = jnp.maximum(before, 0)
            keep[item] = jnp.where(before >= 0, 1.0, 0.0)
            last[k] = item
            return carry

        lax.fori_loop(0, pairs, visit, 0)


def fold(value):
    rows, width = value.shape
    tall = jnp.sum(value.reshape(rows // 8, 8, width), axis=0)
    total = tall[:, :128]
    for c in range(1, width // 128):
        total = total + tall[:, c * 128:(c + 1) * 128]
    return total


def product(side, left, right, block):
    half = lax.dot_general(
        left, block, (((1 - side,), (0,)), ((), ())), preferred_element_type=jnp.float32
    ).astype(jnp.bfloat16)
    return lax.dot_general(
        half, right, (((1,), (side,)), ((), ())), preferred_element_type=jnp.float32
    )


def whole_kernel(
    ops_count, grp_count, pair_dev,
    slots, previous, keep, last, wave_in, diag_in, left_in, right_in,
    residual_out, sigma_out,
    wave, diag, left, right, send_a, blocks_a, out_b, pieces_b, send_c, blocks_c,
    out_d, pieces_d, run, residual, half, sigma, stats, all_stats,
    load_sem, own_sem, send_sem, recv_sem,
):
    o, g = lax.axis_index("ops"), lax.axis_index("grp")
    me = o * grp_count + g
    devices = ops_count * grp_count
    pairs = devices * pair_dev
    sectors, rows, width = wave.shape
    cols = width // grp_count
    wide = jnp.float32
    far_first = sorted(range(grp_count), key=lambda s: -min(s, grp_count - s))
    my_cols = pl.ds(pl.multiple_of(g * cols, cols), cols)

    def each_peer(visit):
        for dg in far_first:

            def step(do, carry, dg=dg):
                visit(lax.rem(o + do, ops_count), lax.rem(g + dg, grp_count))
                return carry

            lax.fori_loop(1 if dg == 0 else 0, ops_count, step, 0)

    def place(ref, side, at_o, at_g, first=0, count=rows):
        return ref.at[
            side, :,
            pl.ds(pl.multiple_of(at_o * rows + first, count), count),
            pl.ds(pl.multiple_of(at_g * cols, cols), cols),
        ]

    def send(group, source, target, to_o, to_g):
        pltpu.make_async_remote_copy(
            src_ref=source, dst_ref=target,
            send_sem=send_sem.at[group], recv_sem=recv_sem.at[group],
            device_id=(to_o, to_g), device_id_type=MESH,
        ).start()

    def whole_of(group, like):
        return pltpu.make_async_remote_copy(
            src_ref=like, dst_ref=like,
            send_sem=send_sem.at[group], recv_sem=recv_sem.at[group],
            device_id=(lax.rem(o + 1, ops_count), g), device_id_type=MESH,
        )

    loads = [
        pltpu.make_async_copy(wave_in, wave, load_sem.at[0]),
        pltpu.make_async_copy(left_in, left, load_sem.at[1]),
        pltpu.make_async_copy(right_in, right, load_sem.at[2]),
        pltpu.make_async_copy(diag_in.at[:, :, my_cols], diag, load_sem.at[3]),
    ]
    for load in loads:
        load.start()
    barrier = pltpu.get_barrier_semaphore()
    each_peer(
        lambda to_o, to_g: pl.semaphore_signal(
            barrier, inc=1, device_id=(to_o, to_g), device_id_type=MESH
        )
    )

    loads[0].wait()

    def stage(side):
        for to in range(ops_count):
            for j in range(pair_dev):
                pair = (to * grp_count + g) * pair_dev + j
                send_a[side, to, j] = wave[slots[side * pairs + pair]]

    fetch_groups, own = (0, 1), []
    stage(0)
    pl.semaphore_wait(barrier, devices - 1)
    my_rows = pl.ds(pl.multiple_of(o * rows, rows), rows)
    for side in range(2):
        if side == 1:
            stage(1)

        def fetch(do, carry, side=side):
            to = lax.rem(o + do, ops_count)
            send(fetch_groups[side], send_a.at[side, to], blocks_a.at[side, :, my_rows, :], to, g)
            return carry

        lax.fori_loop(1, ops_count, fetch, 0)
        own.append(
            pltpu.make_async_copy(
                send_a.at[side, o], blocks_a.at[side, :, my_rows, :], own_sem.at[side]
            )
        )
        own[side].start()

    loads[3].wait()
    zero = jnp.zeros((8, 128), wide)

    def tally(k, carry):
        value = wave[k, :, my_cols].astype(wide)
        square = value * value
        return carry[0] + fold(diag[k] * square), carry[1] + fold(square)

    top, norm = lax.fori_loop(0, sectors, tally, (zero, zero), unroll=2)
    loads[1].wait()
    loads[2].wait()

    def arrive(group, like):
        whole_of(group, like).wait_recv()

    def leave(group, like):
        whole_of(group, like).wait_send()

    fetch_like = [blocks_a.at[s, :, pl.ds(0, (ops_count - 1) * rows), :] for s in range(2)]
    others = pl.ds(0, (devices - 1) * pair_dev)
    short = rows // 2
    parts = [(h * short, short) for h in range(2)]
    stats_like = all_stats.at[pl.ds(0, devices - 1)]
    my_pairs = pl.ds(me * pair_dev, pair_dev)
    first_b, first_c, first_d, stats_group = 2, 5, 9, 12

    def cut(ref, side, which, part):
        return ref.at[side, which, pl.ds(*part)]

    def scatter(side, group, out, pieces, part):
        copy = pltpu.make_async_copy(
            place(out, side, o, g, *part), cut(pieces, side, my_pairs, part), own_sem.at[group]
        )
        copy.start()
        each_peer(
            lambda to_o, to_g: send(
                group, place(out, side, to_o, to_g, *part),
                cut(pieces, side, my_pairs, part), to_o, to_g,
            )
        )
        return copy

    def scatter_all(side, first_group, out, pieces):
        if side == 0:
            return [scatter(0, first_group, out, pieces, (0, rows))]
        return [scatter(1, first_group + 1 + h, out, pieces, parts[h]) for h in range(2)]

    def chain(pieces, side, part):
        at = pl.ds(*part)

        def visit(p, carry):
            item = side * pairs + p
            value = pieces[side, p, at].astype(wide)
            run[item, at] = value + keep[item] * run[previous[item], at]
            return carry

        lax.fori_loop(0, pairs, visit, 0, unroll=4)

    scattered = []
    for side in range(2):
        arrive(fetch_groups[side], fetch_like[side])
        own[side].wait()
        if side == 0:
            out_f = []
            for j in range(pair_dev):
                value = product(0, left[j], right[j], blocks_a[0, j])
                out_b[0, j] = value.astype(jnp.bfloat16)
                out_f.append(value)
        else:
            for j in range(pair_dev):
                value = product(1, left[j], right[j], blocks_a[1, j])
                out_b[1, j] = value.astype(jnp.bfloat16)
                top = top + fold(blocks_a[0, j].astype(wide) * value)
                top = top + fold(blocks_a[1, j].astype(wide) * out_f[j])
            stats[0] = top
            stats[1] = norm
            own_stats = pltpu.make_async_copy(stats, all_stats.at[me], own_sem.at[stats_group])
            own_stats.start()
            each_peer(lambda to_o, to_g: send(stats_group, stats, all_stats.at[me], to_o, to_g))
        scattered += scatter_all(side, first_b, out_b, pieces_b)

    scattered[0].wait()
    arrive(first_b, cut(pieces_b, 0, others, (0, rows)))
    run[0] = jnp.zeros((rows, cols), wide)
    chain(pieces_b, 0, (0, rows))
    own_stats.wait()
    arrive(stats_group, stats_like)
    sums = jnp.sum(all_stats[...], axis=0)
    rayleigh = jnp.sum(sums[0]) / jnp.sum(sums[1])

    returned = {}
    for h, part in enumerate(parts):
        scattered[1 + h].wait()
        arrive(first_b + 1 + h, cut(pieces_b, 1, others, part))
        chain(pieces_b, 1, part)
        at = pl.ds(*part)

        def finish(k, carry, at=at):
            value = (diag[k, at] - rayleigh) * wave[k, at, my_cols].astype(wide)
            value = value + run[last[k], at]
            residual[k, at] = value
            half[k, at] = value.astype(jnp.bfloat16)
            return carry

        lax.fori_loop(0, sectors, finish, 0, unroll=4)
        for side in range(2):
            group = first_c + 2 * h + side

            def hand_out(p, carry, side=side, at=at):
                send_c[side, p, at] = half[slots[side * pairs + p], at]
                return carry

            lax.fori_loop(0, pairs, hand_out, 0, unroll=8)
            target = place(blocks_c, side, o, g, *part)

            def collect(to_o, to_g, side=side, group=group, part=part, target=target):
                to = to_o * grp_count + to_g
                which = pl.ds(to * pair_dev, pair_dev)
                send(group, cut(send_c, side, which, part), target, to_o, to_g)

            each_peer(collect)
            returned[side, h] = pltpu.make_async_copy(
                cut(send_c, side, my_pairs, part), target, own_sem.at[group]
            )
            returned[side, h].start()
    residual_copy = pltpu.make_async_copy(residual, residual_out, load_sem.at[0])
    residual_copy.start()
    scattered = []
    for side in range(2):
        for h, part in enumerate(parts):
            returned[side, h].wait()
            arrive(first_c + 2 * h + side, cut(send_c, side, others, part))
        for j in range(pair_dev):
            value = product(side, left[j], right[j], blocks_c[side, j])
            out_d[side, j] = value.astype(jnp.bfloat16)
        scattered += scatter_all(side, first_d, out_d, pieces_d)
    scattered[0].wait()
    arrive(first_d, cut(pieces_d, 0, others, (0, rows)))
    run[0] = jnp.zeros((rows, cols), wide)
    chain(pieces_d, 0, (0, rows))
    sigma_copies = []
    for h, part in enumerate(parts):
        scattered[1 + h].wait()
        arrive(first_d + 1 + h, cut(pieces_d, 1, others, part))
        chain(pieces_d, 1, part)
        at = pl.ds(*part)

        def close(k, carry, at=at):
            sigma[k, at] = diag[k, at] * half[k, at].astype(wide) + run[last[k], at]
            return carry

        lax.fori_loop(0, sectors, close, 0, unroll=4)
        copy = pltpu.make_async_copy(sigma.at[:, at], sigma_out.at[:, at], load_sem.at[1 + h])
        copy.start()
        sigma_copies.append(copy)
    for side in range(2):
        leave(side, fetch_like[side])
    for first, pieces in ((first_b, pieces_b), (first_d, pieces_d)):
        leave(first, cut(pieces, 0, others, (0, rows)))
        for h, part in enumerate(parts):
            leave(first + 1 + h, cut(pieces, 1, others, part))
    for h, part in enumerate(parts):
        for side in range(2):
            leave(first_c + 2 * h + side, cut(send_c, side, others, part))
    leave(stats_group, stats_like)
    residual_copy.wait()
    for copy in sigma_copies:
        copy.wait()


def direct_body(wave, diag_energy, left_ops, right_ops, pair_sectors, sector_slot):
    ops_count, grp_count = lax.axis_size("ops"), lax.axis_size("grp")
    sectors, rows, width = wave.shape
    height = rows * ops_count
    pair_dev = left_ops.shape[0]
    pairs = pair_sectors.shape[0]
    cols = width // grp_count
    devices = ops_count * grp_count
    thin, wide = jnp.bfloat16, jnp.float32
    shape = jax.ShapeDtypeStruct
    chains = pl.pallas_call(
        chain_kernel,
        out_shape=(
            shape((2 * pairs,), jnp.int32), shape((2 * pairs,), jnp.int32),
            shape((2 * pairs,), wide), shape((sectors,), jnp.int32),
        ),
        in_specs=[SMEM, SMEM], out_specs=(SMEM,) * 4, name="chain",
    )(pair_sectors.T, sector_slot)
    blocks = (2, pair_dev, height, width)
    pieces = (2, pairs, rows, cols)
    share = (sectors, rows, cols)
    return pl.pallas_call(
        functools.partial(whole_kernel, ops_count, grp_count, pair_dev),
        out_shape=(shape(share, wide), shape(share, wide)),
        in_specs=[SMEM] * 4 + [ANY] * 4, out_specs=(ANY, ANY), name="whole",
        scratch_shapes=[
            pltpu.VMEM(wave.shape, thin), pltpu.VMEM(share, wide),
            pltpu.VMEM(left_ops.shape, thin), pltpu.VMEM(right_ops.shape, thin),
            pltpu.VMEM((2, ops_count, pair_dev, rows, width), thin), pltpu.VMEM(blocks, thin),
            pltpu.VMEM(blocks, thin), pltpu.VMEM(pieces, thin),
            pltpu.VMEM(pieces, thin), pltpu.VMEM(blocks, thin),
            pltpu.VMEM(blocks, thin), pltpu.VMEM(pieces, thin),
            pltpu.VMEM((2 * pairs, rows, cols), wide), pltpu.VMEM(share, wide),
            pltpu.VMEM(share, thin), pltpu.VMEM(share, wide),
            pltpu.VMEM((2, 8, 128), wide), pltpu.VMEM((devices, 2, 8, 128), wide),
            pltpu.SemaphoreType.DMA((4,)), pltpu.SemaphoreType.DMA((13,)),
            pltpu.SemaphoreType.DMA((13,)), pltpu.SemaphoreType.DMA((13,)),
        ],
        compiler_params=pltpu.CompilerParams(
            collective_id=0, has_side_effects=True, vmem_limit_bytes=63 << 20
        ),
    )(*chains, wave, diag_energy, left_ops, right_ops)


def segment_total(received, targets, sectors):
    choose = (targets[None, :] == jnp.arange(sectors, dtype=jnp.int32)[:, None]).astype(jnp.float32)
    return jnp.dot(
        choose, received, precision=lax.Precision.HIGHEST, preferred_element_type=jnp.float32
    )


def apply_pairs(vector, left_ops, right_ops, wanted):
    ops_count = lax.axis_size("ops")
    sectors, rows_here, block_width = vector.shape
    pair_dev = left_ops.shape[0]
    cell_count = rows_here * block_width
    outgoing = jnp.take(vector, wanted.reshape(-1), axis=0).reshape(
        ops_count, pair_dev * 2, rows_here, block_width
    )
    fetched = lax.all_to_all(outgoing, "ops", split_axis=0, concat_axis=2, tiled=True)
    inner_half = jnp.einsum(
        "pij,pjk->pik", left_ops, fetched[:, 0], preferred_element_type=jnp.float32
    ).astype(jnp.bfloat16)
    forward = jnp.einsum("pik,pkl->pil", inner_half, right_ops, preferred_element_type=jnp.float32)
    flipped = jnp.einsum(
        "pji,pjk->pik", left_ops, fetched[:, 1], preferred_element_type=jnp.float32
    ).astype(jnp.bfloat16)
    adjoint = jnp.einsum("pik,plk->pil", flipped, right_ops, preferred_element_type=jnp.float32)
    forward_parts = lax.all_to_all(
        forward.reshape(pair_dev, ops_count, rows_here, block_width),
        "ops",
        split_axis=1,
        concat_axis=1,
        tiled=True,
    )
    adjoint_parts = lax.all_to_all(
        adjoint.reshape(pair_dev, ops_count, rows_here, block_width),
        "ops",
        split_axis=1,
        concat_axis=1,
        tiled=True,
    )
    summed = segment_total(
        forward_parts.reshape(-1, cell_count), wanted[:, :, 1].T.reshape(-1), sectors
    )
    summed = summed + segment_total(
        adjoint_parts.reshape(-1, cell_count), wanted[:, :, 0].T.reshape(-1), sectors
    )
    return summed.reshape(sectors, rows_here, block_width)


def reduce_group(partial_value):
    return lax.psum_scatter(partial_value, "grp", scatter_dimension=2, tiled=True)


def collective_body(wave, diag_energy, left_ops, right_ops, pair_sectors, sector_slot):
    ops_count = lax.axis_size("ops")
    grp_count = lax.axis_size("grp")
    pair_dev = left_ops.shape[0]
    block_width = wave.shape[2]
    stored = jnp.take(sector_slot, pair_sectors, axis=0).reshape(ops_count, grp_count, pair_dev, 2)
    wanted = lax.dynamic_index_in_dim(stored, lax.axis_index("grp"), 1, keepdims=False)
    column_share = block_width // grp_count
    column_start = lax.axis_index("grp") * column_share
    applied_sum = reduce_group(apply_pairs(wave, left_ops, right_ops, wanted))
    wave_wide = wave.astype(jnp.float32)
    diag_share = lax.dynamic_slice_in_dim(diag_energy, column_start, column_share, 2)
    wave_share = lax.dynamic_slice_in_dim(wave_wide, column_start, column_share, 2)
    applied = diag_share * wave_share + applied_sum
    products = lax.psum(
        (jnp.sum(wave_share * applied), jnp.sum(wave_share * wave_share)), ("ops", "grp")
    )
    rayleigh = products[0] / products[1]
    residual = applied - rayleigh * wave_share
    residual_half = residual.astype(jnp.bfloat16)
    full_half = lax.all_gather(residual_half, "grp", axis=2, tiled=True)
    second = reduce_group(apply_pairs(full_half, left_ops, right_ops, wanted))
    sigma_out = diag_share * residual_half.astype(jnp.float32) + second
    return (residual, sigma_out)


def solution(mesh):
    rows_tile, lane_tile, most_peers = 32, 128, 64

    def body(wave, diag_energy, left_ops, right_ops, pair_sectors, sector_slot):
        rows, width = wave.shape[1:]
        fits = rows % rows_tile == 0 and width % (lane_tile * mesh.shape["grp"]) == 0
        chosen = direct_body if fits and mesh.size <= most_peers else collective_body
        return chosen(wave, diag_energy, left_ops, right_ops, pair_sectors, sector_slot)

    return jax.shard_map(
        body,
        mesh=mesh,
        in_specs=(
            P(None, "ops", None),
            P(None, "ops", None),
            P(("ops", "grp"), None, None),
            P(("ops", "grp"), None, None),
            P(),
            P(),
        ),
        out_specs=(P(None, "ops", "grp"), P(None, "ops", "grp")),
        check_vma=False,
    )
```

```python
import functools

import jax
import jax.numpy as jnp
from jax import lax
from jax.experimental import pallas as pl
from jax.experimental.pallas import tpu as pltpu
from jax.sharding import PartitionSpec as P

MESH = pl.DeviceIdType.MESH
VMEM = pl.BlockSpec(memory_space=pltpu.VMEM)
SMEM = pl.BlockSpec(memory_space=pltpu.SMEM)
ANY = pl.BlockSpec(memory_space=pl.ANY)


def fold(value):
    rows, width = value.shape
    tall = jnp.sum(value.reshape(rows // 8, 8, width), axis=0)
    total = tall[:, :128]
    for c in range(1, width // 128):
        total = total + tall[:, c * 128:(c + 1) * 128]
    return total


def product(side, left, right, block):
    half = lax.dot_general(
        left, block, (((1 - side,), (0,)), ((), ())), preferred_element_type=jnp.float32
    ).astype(jnp.bfloat16)
    return lax.dot_general(
        half, right, (((1,), (side,)), ((), ())), preferred_element_type=jnp.float32
    )


def whole_kernel(
    ops_count, grp_count, pair_dev,
    pair_sides, sector_slot, wave_in, diag_in, left_in, right_in,
    residual_out, sigma_out,
    wave, diag, left, right, send_a, blocks_a, out_b, pieces_b, send_c, blocks_c,
    out_d, pieces_d, run, residual, half, sigma, stats, all_stats,
    load_sem, own_sem, send_sem, recv_sem, slots, keys, previous, keep, last,
):
    o, g = lax.axis_index("ops"), lax.axis_index("grp")
    me = o * grp_count + g
    devices = ops_count * grp_count
    pairs = devices * pair_dev
    sectors, rows, width = wave.shape
    cols = width // grp_count
    wide = jnp.float32
    far_first = sorted(range(grp_count), key=lambda s: -min(s, grp_count - s))
    my_cols = pl.ds(pl.multiple_of(g * cols, cols), cols)

    def each_peer(visit):
        for dg in far_first:

            def step(do, carry, dg=dg):
                visit(lax.rem(o + do, ops_count), lax.rem(g + dg, grp_count))
                return carry

            lax.fori_loop(1 if dg == 0 else 0, ops_count, step, 0)

    def place(ref, side, at_o, at_g, first=0, count=rows):
        return ref.at[
            side, :,
            pl.ds(pl.multiple_of(at_o * rows + first, count), count),
            pl.ds(pl.multiple_of(at_g * cols, cols), cols),
        ]

    def send(group, source, target, to_o, to_g):
        pltpu.make_async_remote_copy(
            src_ref=source, dst_ref=target,
            send_sem=send_sem.at[group], recv_sem=recv_sem.at[group],
            device_id=(to_o, to_g), device_id_type=MESH,
        ).start()

    def whole_of(group, like):
        return pltpu.make_async_remote_copy(
            src_ref=like, dst_ref=like,
            send_sem=send_sem.at[group], recv_sem=recv_sem.at[group],
            device_id=(lax.rem(o + 1, ops_count), g), device_id_type=MESH,
        )

    loads = [
        pltpu.make_async_copy(wave_in, wave, load_sem.at[0]),
        pltpu.make_async_copy(left_in, left, load_sem.at[1]),
        pltpu.make_async_copy(right_in, right, load_sem.at[2]),
        pltpu.make_async_copy(diag_in.at[:, :, my_cols], diag, load_sem.at[3]),
    ]
    for load in loads:
        load.start()
    barrier = pltpu.get_barrier_semaphore()
    each_peer(
        lambda to_o, to_g: pl.semaphore_signal(
            barrier, inc=1, device_id=(to_o, to_g), device_id_type=MESH
        )
    )

    for side in range(2):

        def name(p, carry, side=side):
            slots[side * pairs + p] = sector_slot[pair_sides[side, p]]
            keys[side * pairs + p] = sector_slot[pair_sides[1 - side, p]]
            return carry

        lax.fori_loop(0, pairs, name, 0, unroll=4)

    loads[0].wait()

    def stage(side):
        for to in range(ops_count):
            for j in range(pair_dev):
                pair = (to * grp_count + g) * pair_dev + j
                send_a[side, to, j] = wave[slots[side * pairs + pair]]

    fetch_groups, own = (0, 1), []
    my_rows = pl.ds(pl.multiple_of(o * rows, rows), rows)

    def fetch_side(side):
        def fetch(do, carry):
            to = lax.rem(o + do, ops_count)
            send(fetch_groups[side], send_a.at[side, to], blocks_a.at[side, :, my_rows, :], to, g)
            return carry

        lax.fori_loop(1, ops_count, fetch, 0)
        own.append(
            pltpu.make_async_copy(
                send_a.at[side, o], blocks_a.at[side, :, my_rows, :], own_sem.at[side]
            )
        )
        own[side].start()

    stage(0)
    pl.semaphore_wait(barrier, devices - 1)
    fetch_side(0)
    stage(1)

    loads[3].wait()
    zero = jnp.zeros((8, 128), wide)

    def tally(k, carry):
        value = wave[k, :, my_cols].astype(wide)
        square = value * value
        return carry[0] + fold(diag[k] * square), carry[1] + fold(square)

    top, norm = lax.fori_loop(0, sectors, tally, (zero, zero), unroll=2)
    loads[1].wait()
    loads[2].wait()

    def arrive(group, like):
        whole_of(group, like).wait_recv()

    def leave(group, like):
        whole_of(group, like).wait_send()

    fetch_like = [blocks_a.at[s, :, pl.ds(0, (ops_count - 1) * rows), :] for s in range(2)]
    others = pl.ds(0, (devices - 1) * pair_dev)
    short = rows // 2
    parts = [(h * short, short) for h in range(2)]
    stats_like = all_stats.at[pl.ds(0, devices - 1)]
    my_pairs = pl.ds(me * pair_dev, pair_dev)
    first_b, first_c, first_d, stats_group = 2, 5, 9, 12

    def cut(ref, side, which, part):
        return ref.at[side, which, pl.ds(*part)]

    def scatter(side, group, out, pieces, part):
        copy = pltpu.make_async_copy(
            place(out, side, o, g, *part), cut(pieces, side, my_pairs, part), own_sem.at[group]
        )
        copy.start()
        each_peer(
            lambda to_o, to_g: send(
                group, place(out, side, to_o, to_g, *part),
                cut(pieces, side, my_pairs, part), to_o, to_g,
            )
        )
        return copy

    def scatter_all(side, first_group, out, pieces):
        if side == 0:
            return [scatter(0, first_group, out, pieces, (0, rows))]
        return [scatter(1, first_group + 1 + h, out, pieces, parts[h]) for h in range(2)]

    def chain(pieces, side, part):
        at = pl.ds(*part)

        def visit(p, carry):
            item = side * pairs + p
            value = pieces[side, p, at].astype(wide)
            run[item, at] = value + keep[item] * run[previous[item], at]
            return carry

        lax.fori_loop(0, pairs, visit, 0, unroll=4)

    scattered = []
    leave(0, fetch_like[0])
    fetch_side(1)
    for side in range(2):
        arrive(fetch_groups[side], fetch_like[side])
        own[side].wait()
        if side == 0:
            out_f = []
            for j in range(pair_dev):
                value = product(0, left[j], right[j], blocks_a[0, j])
                out_b[0, j] = value.astype(jnp.bfloat16)
                out_f.append(value)
        else:
            for j in range(pair_dev):
                value = product(1, left[j], right[j], blocks_a[1, j])
                out_b[1, j] = value.astype(jnp.bfloat16)
                top = top + fold(blocks_a[0, j].astype(wide) * value)
                top = top + fold(blocks_a[1, j].astype(wide) * out_f[j])
            stats[0] = top
            stats[1] = norm
            own_stats = pltpu.make_async_copy(stats, all_stats.at[me], own_sem.at[stats_group])
            own_stats.start()
            each_peer(lambda to_o, to_g: send(stats_group, stats, all_stats.at[me], to_o, to_g))
        scattered += scatter_all(side, first_b, out_b, pieces_b)

    for side in range(2):

        def link(p, carry, side=side):
            item = side * pairs + p
            key = keys[item]

            def look(other, found):
                return jnp.where((keys[other] == key) & (other < item), other, found)

            before = lax.fori_loop(0, (side + 1) * pairs, look, -1, unroll=16)
            previous[item] = jnp.maximum(before, 0)
            keep[item] = jnp.where(before >= 0, 1.0, 0.0)
            return carry

        lax.fori_loop(0, pairs, link, 0)

    def close_chain(k, carry):
        def look(other, found):
            return jnp.where(keys[other] == k, other, found)

        last[k] = lax.fori_loop(0, 2 * pairs, look, 0, unroll=16)
        return carry

    lax.fori_loop(0, sectors, close_chain, 0)
    scattered[0].wait()
    arrive(first_b, cut(pieces_b, 0, others, (0, rows)))
    run[0] = jnp.zeros((rows, cols), wide)
    chain(pieces_b, 0, (0, rows))
    own_stats.wait()
    arrive(stats_group, stats_like)
    sums = jnp.sum(all_stats[...], axis=0)
    rayleigh = jnp.sum(sums[0]) / jnp.sum(sums[1])

    returned = {}
    for h, part in enumerate(parts):
        scattered[1 + h].wait()
        arrive(first_b + 1 + h, cut(pieces_b, 1, others, part))
        chain(pieces_b, 1, part)
        at = pl.ds(*part)

        def finish(k, carry, at=at):
            value = (diag[k, at] - rayleigh) * wave[k, at, my_cols].astype(wide)
            value = value + run[last[k], at]
            residual[k, at] = value
            half[k, at] = value.astype(jnp.bfloat16)
            return carry

        lax.fori_loop(0, sectors, finish, 0, unroll=4)
        for side in range(2):
            group = first_c + 2 * h + side

            def hand_out(p, carry, side=side, at=at):
                send_c[side, p, at] = half[slots[side * pairs + p], at]
                return carry

            lax.fori_loop(0, pairs, hand_out, 0, unroll=8)
            target = place(blocks_c, side, o, g, *part)

            def collect(to_o, to_g, side=side, group=group, part=part, target=target):
                to = to_o * grp_count + to_g
                which = pl.ds(to * pair_dev, pair_dev)
                send(group, cut(send_c, side, which, part), target, to_o, to_g)

            each_peer(collect)
            returned[side, h] = pltpu.make_async_copy(
                cut(send_c, side, my_pairs, part), target, own_sem.at[group]
            )
            returned[side, h].start()
    residual_copy = pltpu.make_async_copy(residual, residual_out, load_sem.at[0])
    residual_copy.start()
    scattered = []
    for side in range(2):
        for h, part in enumerate(parts):
            returned[side, h].wait()
            arrive(first_c + 2 * h + side, cut(send_c, side, others, part))
        for j in range(pair_dev):
            value = product(side, left[j], right[j], blocks_c[side, j])
            out_d[side, j] = value.astype(jnp.bfloat16)
        scattered += scatter_all(side, first_d, out_d, pieces_d)
    scattered[0].wait()
    arrive(first_d, cut(pieces_d, 0, others, (0, rows)))
    run[0] = jnp.zeros((rows, cols), wide)
    chain(pieces_d, 0, (0, rows))
    sigma_copies = []
    for h, part in enumerate(parts):
        scattered[1 + h].wait()
        arrive(first_d + 1 + h, cut(pieces_d, 1, others, part))
        chain(pieces_d, 1, part)
        at = pl.ds(*part)

        def close(k, carry, at=at):
            sigma[k, at] = diag[k, at] * half[k, at].astype(wide) + run[last[k], at]
            return carry

        lax.fori_loop(0, sectors, close, 0, unroll=4)
        copy = pltpu.make_async_copy(sigma.at[:, at], sigma_out.at[:, at], load_sem.at[1 + h])
        copy.start()
        sigma_copies.append(copy)
    leave(1, fetch_like[1])
    for first, pieces in ((first_b, pieces_b), (first_d, pieces_d)):
        leave(first, cut(pieces, 0, others, (0, rows)))
        for h, part in enumerate(parts):
            leave(first + 1 + h, cut(pieces, 1, others, part))
    for h, part in enumerate(parts):
        for side in range(2):
            leave(first_c + 2 * h + side, cut(send_c, side, others, part))
    leave(stats_group, stats_like)
    residual_copy.wait()
    for copy in sigma_copies:
        copy.wait()


def direct_body(wave, diag_energy, left_ops, right_ops, pair_sectors, sector_slot):
    ops_count, grp_count = lax.axis_size("ops"), lax.axis_size("grp")
    sectors, rows, width = wave.shape
    height = rows * ops_count
    pair_dev = left_ops.shape[0]
    pairs = pair_sectors.shape[0]
    cols = width // grp_count
    devices = ops_count * grp_count
    thin, wide = jnp.bfloat16, jnp.float32
    shape = jax.ShapeDtypeStruct
    blocks = (2, pair_dev, height, width)
    pieces = (2, pairs, rows, cols)
    share = (sectors, rows, cols)
    return pl.pallas_call(
        functools.partial(whole_kernel, ops_count, grp_count, pair_dev),
        out_shape=(shape(share, wide), shape(share, wide)),
        in_specs=[SMEM] * 2 + [ANY] * 4, out_specs=(ANY, ANY), name="whole",
        scratch_shapes=[
            pltpu.VMEM(wave.shape, thin), pltpu.VMEM(share, wide),
            pltpu.VMEM(left_ops.shape, thin), pltpu.VMEM(right_ops.shape, thin),
            pltpu.VMEM((2, ops_count, pair_dev, rows, width), thin), pltpu.VMEM(blocks, thin),
            pltpu.VMEM(blocks, thin), pltpu.VMEM(pieces, thin),
            pltpu.VMEM(pieces, thin), pltpu.VMEM(blocks, thin),
            pltpu.VMEM(blocks, thin), pltpu.VMEM(pieces, thin),
            pltpu.VMEM((2 * pairs, rows, cols), wide), pltpu.VMEM(share, wide),
            pltpu.VMEM(share, thin), pltpu.VMEM(share, wide),
            pltpu.VMEM((2, 8, 128), wide), pltpu.VMEM((devices, 2, 8, 128), wide),
            pltpu.SemaphoreType.DMA((4,)), pltpu.SemaphoreType.DMA((13,)),
            pltpu.SemaphoreType.DMA((13,)), pltpu.SemaphoreType.DMA((13,)),
            pltpu.SMEM((2 * pairs,), jnp.int32), pltpu.SMEM((2 * pairs,), jnp.int32),
            pltpu.SMEM((2 * pairs,), jnp.int32), pltpu.SMEM((2 * pairs,), wide),
            pltpu.SMEM((sectors,), jnp.int32),
        ],
        compiler_params=pltpu.CompilerParams(
            collective_id=0, has_side_effects=True, vmem_limit_bytes=63 << 20
        ),
    )(pair_sectors.T, sector_slot, wave, diag_energy, left_ops, right_ops)


def segment_total(received, targets, sectors):
    choose = (targets[None, :] == jnp.arange(sectors, dtype=jnp.int32)[:, None]).astype(jnp.float32)
    return jnp.dot(
        choose, received, precision=lax.Precision.HIGHEST, preferred_element_type=jnp.float32
    )


def apply_pairs(vector, left_ops, right_ops, wanted):
    ops_count = lax.axis_size("ops")
    sectors, rows_here, block_width = vector.shape
    pair_dev = left_ops.shape[0]
    cell_count = rows_here * block_width
    outgoing = jnp.take(vector, wanted.reshape(-1), axis=0).reshape(
        ops_count, pair_dev * 2, rows_here, block_width
    )
    fetched = lax.all_to_all(outgoing, "ops", split_axis=0, concat_axis=2, tiled=True)
    inner_half = jnp.einsum(
        "pij,pjk->pik", left_ops, fetched[:, 0], preferred_element_type=jnp.float32
    ).astype(jnp.bfloat16)
    forward = jnp.einsum("pik,pkl->pil", inner_half, right_ops, preferred_element_type=jnp.float32)
    flipped = jnp.einsum(
        "pji,pjk->pik", left_ops, fetched[:, 1], preferred_element_type=jnp.float32
    ).astype(jnp.bfloat16)
    adjoint = jnp.einsum("pik,plk->pil", flipped, right_ops, preferred_element_type=jnp.float32)
    forward_parts = lax.all_to_all(
        forward.reshape(pair_dev, ops_count, rows_here, block_width),
        "ops",
        split_axis=1,
        concat_axis=1,
        tiled=True,
    )
    adjoint_parts = lax.all_to_all(
        adjoint.reshape(pair_dev, ops_count, rows_here, block_width),
        "ops",
        split_axis=1,
        concat_axis=1,
        tiled=True,
    )
    summed = segment_total(
        forward_parts.reshape(-1, cell_count), wanted[:, :, 1].T.reshape(-1), sectors
    )
    summed = summed + segment_total(
        adjoint_parts.reshape(-1, cell_count), wanted[:, :, 0].T.reshape(-1), sectors
    )
    return summed.reshape(sectors, rows_here, block_width)


def reduce_group(partial_value):
    return lax.psum_scatter(partial_value, "grp", scatter_dimension=2, tiled=True)


def collective_body(wave, diag_energy, left_ops, right_ops, pair_sectors, sector_slot):
    ops_count = lax.axis_size("ops")
    grp_count = lax.axis_size("grp")
    pair_dev = left_ops.shape[0]
    block_width = wave.shape[2]
    stored = jnp.take(sector_slot, pair_sectors, axis=0).reshape(ops_count, grp_count, pair_dev, 2)
    wanted = lax.dynamic_index_in_dim(stored, lax.axis_index("grp"), 1, keepdims=False)
    column_share = block_width // grp_count
    column_start = lax.axis_index("grp") * column_share
    applied_sum = reduce_group(apply_pairs(wave, left_ops, right_ops, wanted))
    wave_wide = wave.astype(jnp.float32)
    diag_share = lax.dynamic_slice_in_dim(diag_energy, column_start, column_share, 2)
    wave_share = lax.dynamic_slice_in_dim(wave_wide, column_start, column_share, 2)
    applied = diag_share * wave_share + applied_sum
    products = lax.psum(
        (jnp.sum(wave_share * applied), jnp.sum(wave_share * wave_share)), ("ops", "grp")
    )
    rayleigh = products[0] / products[1]
    residual = applied - rayleigh * wave_share
    residual_half = residual.astype(jnp.bfloat16)
    full_half = lax.all_gather(residual_half, "grp", axis=2, tiled=True)
    second = reduce_group(apply_pairs(full_half, left_ops, right_ops, wanted))
    sigma_out = diag_share * residual_half.astype(jnp.float32) + second
    return (residual, sigma_out)


def solution(mesh):
    rows_tile, lane_tile, most_peers = 32, 128, 64

    def body(wave, diag_energy, left_ops, right_ops, pair_sectors, sector_slot):
        rows, width = wave.shape[1:]
        fits = rows % rows_tile == 0 and width % (lane_tile * mesh.shape["grp"]) == 0
        chosen = direct_body if fits and mesh.size <= most_peers else collective_body
        return chosen(wave, diag_energy, left_ops, right_ops, pair_sectors, sector_slot)

    return jax.shard_map(
        body,
        mesh=mesh,
        in_specs=(
            P(None, "ops", None),
            P(None, "ops", None),
            P(("ops", "grp"), None, None),
            P(("ops", "grp"), None, None),
            P(),
            P(),
        ),
        out_specs=(P(None, "ops", "grp"), P(None, "ops", "grp")),
        check_vma=False,
    )
```
